32 devices in a mesh: frames: 8 (over z, x), mp: 4 (over y, core).
Axes of the slice: x: 2, y: 2, z: 4, core: 2. Of those that a mesh axis runs over, the one named last changes fastest.
Arguments:
- features: bfloat16 [1024, 512], P('frames'), may hold values from -32 to 32
- logit_weight: bfloat16 [512, 640], replicated, may hold values from -1 to 1
- gumbel_perturbation: float32 [1024, 640], P('frames'), may hold values from -3 to 12
- codebook: bfloat16 [640, 384], replicated, may hold values from -6 to 6
- project_weight: bfloat16 [768, 768], P(None, 'mp'), may hold values from -0.21875 to 0.21875
- context: bfloat16 [1024, 768], P('frames', 'mp'), may hold values from -6 to 6
- distractors: int32 [1024, 100], P('frames'), may hold values from 0 to 1023, as said below
- masked: int32 [1024], P('frames'), may hold values from 0 to 1
Outputs:
- scores: float32 [1024, 101], P('frames')
- loss: float32 [], replicated
- diversity: float32 [], replicated
The draws below stay inside these ranges and needn't reach their ends.
Inputs may be any that keep to these rules, and one draw needn't show every extreme that they name: `distractors`: the distractor of a frame in shard s (frames s * 128 to s * 128 + 127) lies in shard s + o modulo 1024 // 128, with 1 <= |o| <= 3.
All inputs are finite; a program needn't handle non-finite values.
Results may differ from the reference program's by a relative error of at most 0.0049.
Values may be sent and summed in bfloat16 or wider, within the bound.
A program may use at most 64 MiB of HBM per device.

```python
import math
import jax
import jax.numpy as jnp
from jax import lax

FEAT = 512
V = 320
DQ = 768
G = 2
NEG = 100
REACH = 3
TOK_DEV = 128
TOKENS = 1024


def shared_weight(key):
    return jax.random.normal(jax.random.fold_in(key, 11), (FEAT, G * V), jnp.float32) / math.sqrt(FEAT)


def draw_logit_weight(key, part):
    return jnp.clip(shared_weight(key), -1.0, 1.0).astype(jnp.bfloat16)


def draw_features(key, part):
    noise = jax.random.normal(jax.random.fold_in(key, 12), (TOKENS, FEAT), jnp.float32)
    drift = jax.random.normal(jax.random.fold_in(key, 13), (FEAT,), jnp.float32)
    ramp = (2.0 * (jnp.arange(TOKENS, dtype=jnp.float32) + 0.5) / TOKENS - 1.0)[:, None]
    base = noise + 2.0 * ramp * drift[None, :]
    return jnp.clip(base, -32.0, 32.0).astype(jnp.bfloat16)


def draw_gumbel_perturbation(key, part):
    return jnp.clip(jax.random.gumbel(jax.random.fold_in(key, 21), (TOKENS, G * V), jnp.float32), -3.0, 12.0)


def draw_distractors(key, part):
    shards = TOKENS // TOK_DEV
    shard = jnp.arange(TOKENS, dtype=jnp.int32) // TOK_DEV
    choose = jax.random.randint(jax.random.fold_in(key, 31), (TOKENS, NEG), 0, 2 * REACH)
    offset = jnp.where(choose < REACH, choose + 1, REACH - 1 - choose)
    source = (shard[:, None] + offset + shards) % shards
    within = jax.random.randint(jax.random.fold_in(key, 32), (TOKENS, NEG), 0, TOK_DEV)
    return (source * TOK_DEV + within).astype(jnp.int32)


def draw_masked(key, part):
    draw_value = jax.random.randint(jax.random.fold_in(key, 41), (TOKENS,), 0, 1000)
    level = 250 + 500 * jnp.arange(TOKENS, dtype=jnp.int32) // TOKENS
    return (draw_value < level).astype(jnp.int32)


def shard_levels(rng, dims, split, smallest, high):
    factor_of = 1.0
    for dim, shards_of in split:
        heights = jax.random.uniform(jax.random.fold_in(jax.random.fold_in(rng, 6), dim), (shards_of,), jnp.float32, smallest / len(split), high / len(split))
        factor_of = factor_of * jnp.repeat(jnp.exp(heights), dims[dim] // shards_of).reshape((-1,) + (1,) * (len(dims) - 1 - dim))
    return factor_of


def centred(own_key, dims, scale, reach, cuts=(), kind=jnp.bfloat16):
    values = jax.random.normal(own_key, dims, jnp.float32) * scale
    if len(cuts) > 0:
        values = shard_levels(own_key, dims, cuts, -0.22, 0.18) * values
    return jnp.clip(values, min=-reach, max=reach).astype(kind)


def setup_inputs(seed: int = 0) -> dict:
    key_list = jax.random.split(jax.random.key(seed), 9)
    return {
        "features": draw_features(jax.random.fold_in(key_list[8], 71), 0),
        "logit_weight": draw_logit_weight(jax.random.fold_in(key_list[8], 71), 0),
        "gumbel_perturbation": draw_gumbel_perturbation(jax.random.fold_in(key_list[8], 71), 0),
        "codebook": centred(key_list[3], (G * V, DQ // G), 1.0, 6.0),
        "project_weight": centred(key_list[4], (DQ, DQ), DQ ** -0.5, 0.21875, ((1, 4),)),
        "context": centred(key_list[5], (TOKENS, DQ), 1.0, 6.0, ((0, 8), (1, 4))),
        "distractors": draw_distractors(jax.random.fold_in(key_list[8], 71), 0),
        "masked": draw_masked(jax.random.fold_in(key_list[8], 71), 0),
    }


gumbel_softness = 2.0
logit_softness = 0.1
norm_epsilon = 1e-06

def grouped_softmax(values):
    count = values.shape[0]
    shaped = values.reshape(count, G, -1)
    top = lax.optimization_barrier(jnp.max(shaped, axis=2, keepdims=True))
    expd = jnp.exp(shaped - top)
    return (expd / lax.optimization_barrier(jnp.sum(expd, axis=2, keepdims=True))).reshape(count, -1)

def reference(features, logit_weight, gumbel_perturbation, codebook, project_weight, context, distractors, masked):
    codeword_logits = jnp.dot(features.astype(jnp.float32), logit_weight.astype(jnp.float32), preferred_element_type=jnp.float32)
    clean = grouped_softmax(codeword_logits)
    usage = lax.optimization_barrier(jnp.mean(clean, axis=0)).reshape(G, V)
    perplex = jnp.sum(jnp.exp(-lax.optimization_barrier(jnp.sum(usage * jnp.log(usage + 1e-07), axis=1))))
    diversity = (G * V - perplex) / (G * V)
    soft_assignment = grouped_softmax((codeword_logits + gumbel_perturbation) / gumbel_softness).astype(jnp.bfloat16)
    pieces = [jnp.dot(soft_assignment[:, g * V:(g + 1) * V].astype(jnp.float32), codebook[g * V:(g + 1) * V].astype(jnp.float32), preferred_element_type=jnp.float32) for g in range(G)]
    codevec = jnp.concatenate(pieces, axis=1).astype(jnp.bfloat16)
    target = jnp.dot(codevec.astype(jnp.float32), project_weight.astype(jnp.float32), preferred_element_type=jnp.float32)
    unit = (target * lax.rsqrt(lax.optimization_barrier(jnp.sum(target * target, axis=1)) + norm_epsilon)[:, None]).astype(jnp.bfloat16)
    ctx_float = context.astype(jnp.float32)
    context_squared = lax.optimization_barrier(jnp.sum(ctx_float * ctx_float, axis=1))
    self_dot = lax.optimization_barrier(jnp.sum(ctx_float * unit.astype(jnp.float32), axis=1))
    block = math.gcd(context.shape[0], 128)
    ctx_blocks = context.reshape(-1, block, DQ)
    idx_blocks = distractors.reshape(-1, block, NEG)

    def one_block(pair):
        ctx_part, idx_part = pair
        taken = unit[idx_part.astype(jnp.int32)].astype(jnp.float32)
        return jnp.einsum('td,tkd->tk', ctx_part.astype(jnp.float32), taken)
    other_dot = lax.map(one_block, (ctx_blocks, idx_blocks)).reshape(-1, NEG)
    inner_products = jnp.concatenate([self_dot[:, None], other_dot], axis=1)
    scores = inner_products * lax.rsqrt(context_squared + norm_epsilon)[:, None] / logit_softness
    cross = jnp.log(lax.optimization_barrier(jnp.sum(jnp.exp(scores), axis=1))) - scores[:, 0]
    loss = jnp.sum(jnp.where(masked == 1, cross, jnp.float32(0.0))) / scores.shape[0]
    return (scores, loss, diversity)
```

```python
import functools

import jax
import jax.numpy as jnp
from jax import lax
from jax.experimental import pallas as pl
from jax.experimental.pallas import tpu as pltpu
from jax.sharding import PartitionSpec as P

V = 320
G = 2
REACH = 3

gumbel_softness = 2.0
logit_softness = 0.1
norm_epsilon = 1e-06

MESH = pl.DeviceIdType.MESH
OFFSETS = tuple(s * o for o in range(1, REACH + 1) for s in (1, -1))
LANES = 128


def group_softmax(values, first):
    low = jnp.float32(-jnp.inf)
    top = jnp.where(
        first,
        jnp.max(jnp.where(first, values, low), axis=1, keepdims=True),
        jnp.max(jnp.where(first, low, values), axis=1, keepdims=True),
    )
    expd = jnp.exp(values - top)
    sum0 = jnp.sum(jnp.where(first, expd, 0.0), axis=1, keepdims=True)
    sum1 = jnp.sum(jnp.where(first, 0.0, expd), axis=1, keepdims=True)
    return expd * jnp.where(first, 1.0 / sum0, 1.0 / sum1)


def kernel(
    shards, parts,
    feat_h, lw_h, gum_h, cb_h, pwt_h, ctxt_h, dist_h, mask_h,
    scores_o, loss_o, div_o,
    feat, lw, gum, cb, pwt, ctxt, dist, mask, load_sem,
    own_t, nb, t_send, t_recv,
    use_all, u_send, u_recv,
    dots_all, d_send, d_recv,
    rows_all, r_send, r_recv,
    ce_all, c_send, c_recv,
):
    own = lax.axis_index("frames")
    part = lax.axis_index("mp")
    count = feat.shape[0]
    neg = dist.shape[0]
    wide = lw.shape[1]

    loads = []
    order = ((feat_h, feat), (lw_h, lw), (gum_h, gum), (cb_h, cb), (pwt_h, pwt), (ctxt_h, ctxt), (dist_h, dist), (mask_h, mask))
    for i, (src, dst) in enumerate(order):
        load = pltpu.make_async_copy(src, dst, load_sem.at[i])
        load.start()
        loads.append(load)

    barrier = pltpu.get_barrier_semaphore()
    for o in range(1, shards):
        pl.semaphore_signal(barrier, inc=1, device_id=(lax.rem(own + o, shards), part), device_id_type=MESH)
    for o in range(1, parts):
        pl.semaphore_signal(barrier, inc=1, device_id=(own, lax.rem(part + o, parts)), device_id_type=MESH)

    loads[0].wait()
    loads[1].wait()
    logits = jnp.dot(feat[...], lw[...], preferred_element_type=jnp.float32)
    first = lax.broadcasted_iota(jnp.int32, (count, wide), 1) < V
    loads[2].wait()
    soft = group_softmax((logits + gum[...]) / gumbel_softness, first)
    loads[3].wait()
    inner = V // LANES * LANES
    outer = -(-V // LANES) * LANES
    piece0 = jnp.dot(
        jnp.where(first, soft, 0.0)[:, :outer].astype(jnp.bfloat16), cb[:outer, :],
        preferred_element_type=jnp.float32,
    ).astype(jnp.bfloat16)
    piece1 = jnp.dot(
        jnp.where(first, 0.0, soft)[:, inner:].astype(jnp.bfloat16), cb[inner:, :],
        preferred_element_type=jnp.float32,
    ).astype(jnp.bfloat16)
    codevec = jnp.concatenate([piece0, piece1], axis=1)
    loads[4].wait()
    target = lax.dot_general(
        pwt[...], codevec, (((1,), (1,)), ((), ())), preferred_element_type=jnp.float32
    )
    own_t[...] = target.astype(jnp.bfloat16)

    pl.semaphore_wait(barrier, shards - 1 + parts - 1)

    sends = []
    for j, o in enumerate(OFFSETS):
        copy = pltpu.make_async_remote_copy(
            src_ref=own_t, dst_ref=nb.at[j], send_sem=t_send.at[j], recv_sem=t_recv.at[j],
            device_id=(lax.rem(own - o + shards, shards), part), device_id_type=MESH,
        )
        copy.start()
        sends.append(copy)

    def spread_frames(buffer, send_sem, recv_sem):
        copies = []
        for o in range(1, shards):
            copy = pltpu.make_async_remote_copy(
                src_ref=buffer.at[own], dst_ref=buffer.at[own], send_sem=send_sem.at[o],
                recv_sem=recv_sem.at[own],
                device_id=(lax.rem(own + o, shards), part), device_id_type=MESH,
            )
            copy.start()
            copies.append(copy)
        return copies

    def await_frames(buffer, send_sem, recv_sem):
        for o in range(1, shards):
            source = lax.rem(own + o, shards)
            pltpu.make_async_remote_copy(
                src_ref=buffer.at[source], dst_ref=buffer.at[source], send_sem=send_sem.at[o],
                recv_sem=recv_sem.at[source],
                device_id=(source, part), device_id_type=MESH,
            ).wait_recv()

    def spread_parts(buffer, send_sem, recv_sem):
        copies = []
        for o in range(1, parts):
            copy = pltpu.make_async_remote_copy(
                src_ref=buffer.at[part], dst_ref=buffer.at[part], send_sem=send_sem.at[o],
                recv_sem=recv_sem.at[part],
                device_id=(own, lax.rem(part + o, parts)), device_id_type=MESH,
            )
            copy.start()
            copies.append(copy)
        return copies

    def await_parts(buffer, send_sem, recv_sem):
        for o in range(1, parts):
            source = lax.rem(part + o, parts)
            pltpu.make_async_remote_copy(
                src_ref=buffer.at[source], dst_ref=buffer.at[source], send_sem=send_sem.at[o],
                recv_sem=recv_sem.at[source],
                device_id=(own, source), device_id_type=MESH,
            ).wait_recv()

    clean = group_softmax(logits, first)
    use_all[own] = jnp.sum(clean, axis=0, keepdims=True)
    sends += spread_frames(use_all, u_send, u_recv)

    loads[5].wait()
    ctx_f = ctxt[...].astype(jnp.float32)
    ctx = ctx_f.T.astype(jnp.bfloat16)
    tgt_f = own_t[...].astype(jnp.float32)
    row_self = jnp.sum(ctx_f * tgt_f, axis=0, keepdims=True)
    row_norm = jnp.sum(tgt_f * tgt_f, axis=0, keepdims=True)
    row_ctx = jnp.sum(ctx_f * ctx_f, axis=0, keepdims=True)
    loads[6].wait()
    loads[7].wait()
    picks = jnp.concatenate(
        [dist[...], jnp.zeros((LANES - neg, count), jnp.int32)], axis=0
    ).astype(jnp.float32).T.astype(jnp.int32)
    owner = picks // count
    local = picks - owner * count
    distance = owner - own
    distance = jnp.where(distance < 0, distance + shards, distance)

    rows = [row_self, row_norm, row_ctx]
    dots = jnp.zeros((count, LANES), jnp.float32)
    for j, o in enumerate(OFFSETS):
        sends[j].wait_recv()
        block = nb[j]
        sims = jnp.dot(ctx, block, preferred_element_type=jnp.float32)
        block_f = block.astype(jnp.float32)
        rows.append(jnp.sum(block_f * block_f, axis=0, keepdims=True))
        taken = jnp.take_along_axis(sims, local, axis=1)
        dots = jnp.where(distance == o % shards, taken, dots)
    rows += [jnp.zeros((1, count), jnp.float32)] * (rows_all.shape[1] - len(rows))
    rows_all[part] = jnp.concatenate(rows, axis=0)
    sends += spread_parts(rows_all, r_send, r_recv)
    dots_all[part] = dots.astype(jnp.bfloat16)
    sends += spread_parts(dots_all, d_send, d_recv)

    await_parts(rows_all, r_send, r_recv)
    rows_sum = rows_all[0]
    for p in range(1, parts):
        rows_sum = rows_sum + rows_all[p]
    inverse = lax.rsqrt(rows_sum + norm_epsilon)
    scale = jnp.zeros((count, LANES), jnp.float32)
    for j, o in enumerate(OFFSETS):
        table = jnp.broadcast_to(inverse[3 + j : 4 + j], (count, LANES))
        taken = jnp.take_along_axis(table, local, axis=1)
        scale = jnp.where(distance == o % shards, taken, scale)

    await_parts(dots_all, d_send, d_recv)
    dots_sum = dots_all[0].astype(jnp.float32)
    for p in range(1, parts):
        dots_sum = dots_sum + dots_all[p].astype(jnp.float32)
    gain = inverse[2:3] / logit_softness
    others = (dots_sum * scale).T[:neg] * gain
    first_row = rows_sum[0:1] * inverse[1:2] * gain
    scores_o[0:1, :] = first_row
    scores_o[1 : neg + 1, :] = others
    total = jnp.exp(first_row) + jnp.sum(jnp.exp(others), axis=0, keepdims=True)
    cross = jnp.log(total) - first_row
    ce_all[own] = jnp.where(mask[...] == 1, cross, 0.0)
    sends += spread_frames(ce_all, c_send, c_recv)

    await_frames(use_all, u_send, u_recv)
    frames_all = count * shards
    usage = use_all[0]
    for s in range(1, shards):
        usage = usage + use_all[s]
    usage = usage / frames_all
    entropy = usage * jnp.log(usage + 1e-07)
    in_first = lax.broadcasted_iota(jnp.int32, (1, wide), 1) < V
    ent0 = jnp.sum(jnp.where(in_first, entropy, 0.0), axis=1, keepdims=True)
    ent1 = jnp.sum(jnp.where(in_first, 0.0, entropy), axis=1, keepdims=True)
    perplex = jnp.exp(-ent0) + jnp.exp(-ent1)
    div_o[0] = jnp.sum((wide - perplex) / wide)

    await_frames(ce_all, c_send, c_recv)
    losses = ce_all[0]
    for s in range(1, shards):
        losses = losses + ce_all[s]
    loss_o[0] = jnp.sum(losses) / frames_all
    for copy in sends:
        copy.wait_send()


def on_device(shards, parts, features, logit_weight, gumbel, codebook, project_weight, context, distractors, masked):
    count, neg = distractors.shape
    width = context.shape[1]
    wide = logit_weight.shape[1]
    bf16, f32 = jnp.bfloat16, jnp.float32
    operands = (
        features, logit_weight, gumbel, codebook, project_weight.T, context.T, distractors.T,
        masked.reshape(1, count),
    )
    dma = pltpu.SemaphoreType.DMA
    scores, loss, diversity = pl.pallas_call(
        functools.partial(kernel, shards, parts),
        out_shape=(
            jax.ShapeDtypeStruct((neg + 1, count), f32),
            jax.ShapeDtypeStruct((1,), f32),
            jax.ShapeDtypeStruct((1,), f32),
        ),
        in_specs=[pl.BlockSpec(memory_space=pl.ANY)] * len(operands),
        out_specs=(
            pl.BlockSpec(memory_space=pltpu.VMEM),
            pl.BlockSpec(memory_space=pltpu.SMEM),
            pl.BlockSpec(memory_space=pltpu.SMEM),
        ),
        scratch_shapes=[pltpu.VMEM(x.shape, x.dtype) for x in operands]
        + [
            dma((len(operands),)),
            pltpu.VMEM((width, count), bf16),
            pltpu.VMEM((2 * REACH, width, count), bf16), dma((2 * REACH,)), dma((2 * REACH,)),
            pltpu.VMEM((shards, 1, wide), f32), dma((shards,)), dma((shards,)),
            pltpu.VMEM((parts, count, LANES), bf16), dma((parts,)), dma((parts,)),
            pltpu.VMEM((parts, 16, count), f32), dma((parts,)), dma((parts,)),
            pltpu.VMEM((shards, 1, count), f32), dma((shards,)), dma((shards,)),
        ],
        compiler_params=pltpu.CompilerParams(collective_id=0, has_side_effects=True),
    )(*operands)
    return scores.T, loss.reshape(()), diversity.reshape(())


def solution(mesh):
    return jax.shard_map(
        functools.partial(on_device, mesh.shape["frames"], mesh.shape["mp"]),
        mesh=mesh,
        in_specs=(
            P("frames", None),
            P(),
            P("frames", None),
            P(),
            P(None, "mp"),
            P("frames", "mp"),
            P("frames", None),
            P("frames"),
        ),
        out_specs=(P("frames", None), P(), P()),
        check_vma=False,
    )
```

```python
import functools

import jax
import jax.numpy as jnp
from jax import lax
from jax.experimental import pallas as pl
from jax.experimental.pallas import tpu as pltpu
from jax.sharding import PartitionSpec as P

V = 320
G = 2
REACH = 3

gumbel_softness = 2.0
logit_softness = 0.1
norm_epsilon = 1e-06

MESH = pl.DeviceIdType.MESH
LANES = 128


def group_softmax(values, first):
    low = jnp.float32(-jnp.inf)
    top = jnp.where(
        first,
        jnp.max(jnp.where(first, values, low), axis=1, keepdims=True),
        jnp.max(jnp.where(first, low, values), axis=1, keepdims=True),
    )
    expd = jnp.exp(values - top)
    sum0 = jnp.sum(jnp.where(first, expd, 0.0), axis=1, keepdims=True)
    sum1 = jnp.sum(jnp.where(first, 0.0, expd), axis=1, keepdims=True)
    return expd * jnp.where(first, 1.0 / sum0, 1.0 / sum1)


def kernel(
    shards, parts,
    feat_h, lw_h, gum_h, cb_h, pwt_h, ctxt_h, dist_h, mask_h,
    scores_o, loss_o, div_o,
    feat, lw, gum, cb, pwt, ctxt, dist, mask, load_sem,
    own_t, nb, t_send, t_recv,
    use_all, u_send, u_recv,
    dots_all, d_send, d_recv,
    rows_all, r_send, r_recv,
    ce_all, c_send, c_recv,
):
    own = lax.axis_index("frames")
    part = lax.axis_index("mp")
    count = feat.shape[0]
    neg = dist.shape[0]
    wide = lw.shape[1]

    loads = []
    order = ((feat_h, feat), (lw_h, lw), (gum_h, gum), (cb_h, cb), (pwt_h, pwt), (ctxt_h, ctxt), (dist_h, dist), (mask_h, mask))
    for i, (src, dst) in enumerate(order):
        load = pltpu.make_async_copy(src, dst, load_sem.at[i])
        load.start()
        loads.append(load)

    barrier = pltpu.get_barrier_semaphore()
    for o in range(1, shards):
        pl.semaphore_signal(barrier, inc=1, device_id=(lax.rem(own + o, shards), part), device_id_type=MESH)
    for o in range(1, parts):
        pl.semaphore_signal(barrier, inc=1, device_id=(own, lax.rem(part + o, parts)), device_id_type=MESH)

    loads[0].wait()
    loads[1].wait()
    logits = jnp.dot(feat[...], lw[...], preferred_element_type=jnp.float32)
    first = lax.broadcasted_iota(jnp.int32, (count, wide), 1) < V
    loads[2].wait()
    soft = group_softmax((logits + gum[...]) / gumbel_softness, first)
    loads[3].wait()
    inner = V // LANES * LANES
    outer = -(-V // LANES) * LANES
    piece0 = jnp.dot(
        jnp.where(first, soft, 0.0)[:, :outer].astype(jnp.bfloat16), cb[:outer, :],
        preferred_element_type=jnp.float32,
    ).astype(jnp.bfloat16)
    piece1 = jnp.dot(
        jnp.where(first, 0.0, soft)[:, inner:].astype(jnp.bfloat16), cb[inner:, :],
        preferred_element_type=jnp.float32,
    ).astype(jnp.bfloat16)
    codevec = jnp.concatenate([piece0, piece1], axis=1)
    loads[4].wait()
    target = lax.dot_general(
        pwt[...], codevec, (((1,), (1,)), ((), ())), preferred_element_type=jnp.float32
    )
    own_t[...] = target.astype(jnp.bfloat16)

    pl.semaphore_wait(barrier, shards - 1 + parts - 1)

    pair = 1 - 2 * lax.rem(own, 2)
    offsets = (pair, 2, -2, 2 + pair, pair - 2, -3 * pair)
    steps = (pair, -2, 2, pair - 2, pair + 2, -3 * pair)
    distances = [lax.rem(o + shards, shards) for o in offsets]

    def hand(src, j, step):
        copy = pltpu.make_async_remote_copy(
            src_ref=src, dst_ref=nb.at[j], send_sem=t_send.at[j], recv_sem=t_recv.at[j],
            device_id=(lax.rem(own + step + shards, shards), part), device_id_type=MESH,
        )
        copy.start()
        return copy

    route = (5, 4, 3, 2, 1, 0)
    arrivals = {j: hand(own_t, j, steps[j]) for j in route}
    sends = list(arrivals.values())

    def spread_frames(buffer, send_sem, recv_sem):
        copies = []
        for o in range(1, shards):
            copy = pltpu.make_async_remote_copy(
                src_ref=buffer.at[own], dst_ref=buffer.at[own], send_sem=send_sem.at[o],
                recv_sem=recv_sem.at[own],
                device_id=(lax.rem(own + o, shards), part), device_id_type=MESH,
            )
            copy.start()
            copies.append(copy)
        return copies

    def await_frames(buffer, send_sem, recv_sem):
        for o in range(1, shards):
            source = lax.rem(own + o, shards)
            pltpu.make_async_remote_copy(
                src_ref=buffer.at[source], dst_ref=buffer.at[source], send_sem=send_sem.at[o],
                recv_sem=recv_sem.at[source],
                device_id=(source, part), device_id_type=MESH,
            ).wait_recv()

    def spread_parts(buffer, send_sem, recv_sem):
        copies = []
        for o in range(1, parts):
            copy = pltpu.make_async_remote_copy(
                src_ref=buffer.at[part], dst_ref=buffer.at[part], send_sem=send_sem.at[o],
                recv_sem=recv_sem.at[part],
                device_id=(own, lax.rem(part + o, parts)), device_id_type=MESH,
            )
            copy.start()
            copies.append(copy)
        return copies

    def await_parts(buffer, send_sem, recv_sem):
        for o in range(1, parts):
            source = lax.rem(part + o, parts)
            pltpu.make_async_remote_copy(
                src_ref=buffer.at[source], dst_ref=buffer.at[source], send_sem=send_sem.at[o],
                recv_sem=recv_sem.at[source],
                device_id=(own, source), device_id_type=MESH,
            ).wait_recv()

    clean = group_softmax(logits, first)
    use_all[own] = jnp.sum(clean, axis=0, keepdims=True)

    loads[5].wait()
    ctx_f = ctxt[...].astype(jnp.float32)
    ctx = ctx_f.T.astype(jnp.bfloat16)
    tgt_f = own_t[...].astype(jnp.float32)
    row_self = jnp.sum(ctx_f * tgt_f, axis=0, keepdims=True)
    row_norm = jnp.sum(tgt_f * tgt_f, axis=0, keepdims=True)
    row_ctx = jnp.sum(ctx_f * ctx_f, axis=0, keepdims=True)
    loads[6].wait()
    loads[7].wait()
    picks = jnp.concatenate(
        [jnp.zeros((1, count), jnp.int32), dist[...], jnp.zeros((LANES - neg - 1, count), jnp.int32)], axis=0
    ).astype(jnp.float32).T.astype(jnp.int32)
    owner = picks // count
    local = picks - owner * count
    distance = owner - own
    distance = jnp.where(distance < 0, distance + shards, distance)

    norms = [None] * len(offsets)
    dots = jnp.zeros((count, LANES), jnp.float32)
    last = 0
    for j in (2, 1, 5, 4, 3, last):
        arrivals[j].wait_recv()
        block = nb[j]
        block_f = block.astype(jnp.float32)
        norms[j] = jnp.sum(block_f * block_f, axis=0, keepdims=True)
        if j == last:
            rows = [row_self, row_norm, row_ctx] + norms
            rows += [jnp.zeros((1, count), jnp.float32)] * (rows_all.shape[1] - len(rows))
            rows_all[part] = jnp.concatenate(rows, axis=0)
            sends += spread_parts(rows_all, r_send, r_recv)
        sims = jnp.dot(ctx, block, preferred_element_type=jnp.float32)
        taken = jnp.take_along_axis(sims, local, axis=1)
        dots = jnp.where(distance == distances[j], taken, dots)
    dots_all[part] = dots.astype(jnp.bfloat16)
    sends += spread_parts(dots_all, d_send, d_recv)
    sends += spread_frames(use_all, u_send, u_recv)

    await_parts(rows_all, r_send, r_recv)
    rows_sum = rows_all[0]
    for p in range(1, parts):
        rows_sum = rows_sum + rows_all[p]
    inverse = lax.rsqrt(rows_sum + norm_epsilon)
    scale = jnp.zeros((count, LANES), jnp.float32)
    for j, d in enumerate(distances):
        table = jnp.broadcast_to(inverse[3 + j : 4 + j], (count, LANES))
        taken = jnp.take_along_axis(table, local, axis=1)
        scale = jnp.where(distance == d, taken, scale)

    await_parts(dots_all, d_send, d_recv)
    dots_sum = dots_all[0].astype(jnp.float32)
    for p in range(1, parts):
        dots_sum = dots_sum + dots_all[p].astype(jnp.float32)
    gain = inverse[2:3] / logit_softness
    row = lax.broadcasted_iota(jnp.int32, (LANES, count), 0)
    first_row = rows_sum[0:1] * inverse[1:2] * gain
    found = jnp.where(row == 0, first_row, (dots_sum * scale).T * gain)
    scores_o[...] = found[: neg + 1]
    total = jnp.sum(jnp.where(row <= neg, jnp.exp(found), 0.0), axis=0, keepdims=True)
    cross = jnp.log(total) - first_row
    ce_all[own] = jnp.where(mask[...] == 1, cross, 0.0)
    sends += spread_frames(ce_all, c_send, c_recv)

    await_frames(use_all, u_send, u_recv)
    frames_all = count * shards
    usage = use_all[0]
    for s in range(1, shards):
        usage = usage + use_all[s]
    usage = usage / frames_all
    entropy = usage * jnp.log(usage + 1e-07)
    in_first = lax.broadcasted_iota(jnp.int32, (1, wide), 1) < V
    ent0 = jnp.sum(jnp.where(in_first, entropy, 0.0), axis=1, keepdims=True)
    ent1 = jnp.sum(jnp.where(in_first, 0.0, entropy), axis=1, keepdims=True)
    perplex = jnp.exp(-ent0) + jnp.exp(-ent1)
    div_o[0] = jnp.sum((wide - perplex) / wide)

    await_frames(ce_all, c_send, c_recv)
    losses = ce_all[0]
    for s in range(1, shards):
        losses = losses + ce_all[s]
    loss_o[0] = jnp.sum(losses) / frames_all
    for copy in sends:
        copy.wait_send()


def on_device(shards, parts, features, logit_weight, gumbel, codebook, project_weight, context, distractors, masked):
    count, neg = distractors.shape
    width = context.shape[1]
    wide = logit_weight.shape[1]
    bf16, f32 = jnp.bfloat16, jnp.float32
    operands = (
        features, logit_weight, gumbel, codebook, project_weight.T, context.T, distractors.T,
        masked.reshape(1, count),
    )
    dma = pltpu.SemaphoreType.DMA
    scores, loss, diversity = pl.pallas_call(
        functools.partial(kernel, shards, parts),
        out_shape=(
            pltpu.VMEM((neg + 1, count), f32),
            pltpu.SMEM((1,), f32),
            pltpu.SMEM((1,), f32),
        ),
        in_specs=[pl.BlockSpec(memory_space=pl.ANY)] * len(operands),
        out_specs=(
            pl.BlockSpec(memory_space=pltpu.VMEM),
            pl.BlockSpec(memory_space=pltpu.SMEM),
            pl.BlockSpec(memory_space=pltpu.SMEM),
        ),
        scratch_shapes=[pltpu.VMEM(x.shape, x.dtype) for x in operands]
        + [
            dma((len(operands),)),
            pltpu.VMEM((width, count), bf16),
            pltpu.VMEM((2 * REACH, width, count), bf16), dma((2 * REACH,)), dma((2 * REACH,)),
            pltpu.VMEM((shards, 1, wide), f32), dma((shards,)), dma((shards,)),
            pltpu.VMEM((parts, count, LANES), bf16), dma((parts,)), dma((parts,)),
            pltpu.VMEM((parts, 16, count), f32), dma((parts,)), dma((parts,)),
            pltpu.VMEM((shards, 1, count), f32), dma((shards,)), dma((shards,)),
        ],
        compiler_params=pltpu.CompilerParams(collective_id=0, has_side_effects=True),
    )(*operands)
    return scores.T, loss.reshape(()), diversity.reshape(())


def solution(mesh):
    return jax.shard_map(
        functools.partial(on_device, mesh.shape["frames"], mesh.shape["mp"]),
        mesh=mesh,
        in_specs=(
            P("frames", None),
            P(),
            P("frames", None),
            P(),
            P(None, "mp"),
            P("frames", "mp"),
            P("frames", None),
            P("frames"),
        ),
        out_specs=(P("frames", None), P(), P()),
        check_vma=False,
    )
```

```python
import functools

import jax
import jax.numpy as jnp
from jax import lax
from jax.experimental import pallas as pl
from jax.experimental.pallas import tpu as pltpu
from jax.sharding import PartitionSpec as P

V = 320
G = 2
REACH = 3

gumbel_softness = 2.0
logit_softness = 0.1
norm_epsilon = 1e-06

MESH = pl.DeviceIdType.MESH
LANES = 128


def group_softmax(values, first):
    low = jnp.float32(-jnp.inf)
    top = jnp.where(
        first,
        jnp.max(jnp.where(first, values, low), axis=1, keepdims=True),
        jnp.max(jnp.where(first, low, values), axis=1, keepdims=True),
    )
    expd = jnp.exp(values - top)
    sum0 = jnp.sum(jnp.where(first, expd, 0.0), axis=1, keepdims=True)
    sum1 = jnp.sum(jnp.where(first, 0.0, expd), axis=1, keepdims=True)
    return expd * jnp.where(first, 1.0 / sum0, 1.0 / sum1)


def kernel(
    shards, parts,
    feat_h, lw_h, gum_h, cb_h, pwt_h, ctxt_h, dist_h, mask_h,
    scores_o, pair_o,
    feat, lw, gum, cb, pwt, ctxt, dist, mask, load_sem,
    own_t, nb, t_send, t_recv,
    use_all, u_send, u_recv,
    dots_all, d_send, d_recv,
    rows_all, r_send, r_recv,
    ce_all, c_send, c_recv,
):
    own = lax.axis_index("frames")
    part = lax.axis_index("mp")
    count = feat.shape[0]
    neg = dist.shape[0]
    wide = lw.shape[1]

    loads = []
    order = ((feat_h, feat), (lw_h, lw), (gum_h, gum), (cb_h, cb), (pwt_h, pwt), (ctxt_h, ctxt), (dist_h, dist), (mask_h, mask))
    for i, (src, dst) in enumerate(order):
        load = pltpu.make_async_copy(src, dst, load_sem.at[i])
        load.start()
        loads.append(load)

    barrier = pltpu.get_barrier_semaphore()
    for o in range(1, shards):
        pl.semaphore_signal(barrier, inc=1, device_id=(lax.rem(own + o, shards), part), device_id_type=MESH)
    for o in range(1, parts):
        pl.semaphore_signal(barrier, inc=1, device_id=(own, lax.rem(part + o, parts)), device_id_type=MESH)

    loads[0].wait()
    loads[1].wait()
    logits = jnp.dot(feat[...], lw[...], preferred_element_type=jnp.float32)
    first = lax.broadcasted_iota(jnp.int32, (count, wide), 1) < V
    loads[2].wait()
    soft = group_softmax((logits + gum[...]) / gumbel_softness, first)
    loads[3].wait()
    inner = V // LANES * LANES
    outer = -(-V // LANES) * LANES
    piece0 = jnp.dot(
        jnp.where(first, soft, 0.0)[:, :outer].astype(jnp.bfloat16), cb[:outer, :],
        preferred_element_type=jnp.float32,
    ).astype(jnp.bfloat16)
    piece1 = jnp.dot(
        jnp.where(first, 0.0, soft)[:, inner:].astype(jnp.bfloat16), cb[inner:, :],
        preferred_element_type=jnp.float32,
    ).astype(jnp.bfloat16)
    codevec = jnp.concatenate([piece0, piece1], axis=1)
    loads[4].wait()
    target = lax.dot_general(
        pwt[...], codevec, (((1,), (1,)), ((), ())), preferred_element_type=jnp.float32
    )
    own_t[...] = target.astype(jnp.bfloat16)

    pl.semaphore_wait(barrier, shards - 1 + parts - 1)

    pair = 1 - 2 * lax.rem(own, 2)
    offsets = (pair, 2, -2, 2 + pair, pair - 2, -3 * pair)
    steps = (pair, -2, 2, pair - 2, pair + 2, -3 * pair)
    distances = [lax.rem(o + shards, shards) for o in offsets]

    def hand(src, j, step):
        copy = pltpu.make_async_remote_copy(
            src_ref=src, dst_ref=nb.at[j], send_sem=t_send.at[j], recv_sem=t_recv.at[j],
            device_id=(lax.rem(own + step + shards, shards), part), device_id_type=MESH,
        )
        copy.start()
        return copy

    route = (5, 4, 3, 2, 1, 0)
    arrivals = {j: hand(own_t, j, steps[j]) for j in route}
    sends = list(arrivals.values())

    def spread_frames(buffer, send_sem, recv_sem):
        copies = []
        for o in range(1, shards):
            copy = pltpu.make_async_remote_copy(
                src_ref=buffer.at[own], dst_ref=buffer.at[own], send_sem=send_sem.at[o],
                recv_sem=recv_sem.at[own],
                device_id=(lax.rem(own + o, shards), part), device_id_type=MESH,
            )
            copy.start()
            copies.append(copy)
        return copies

    def await_frames(buffer, send_sem, recv_sem):
        for o in range(1, shards):
            source = lax.rem(own + o, shards)
            pltpu.make_async_remote_copy(
                src_ref=buffer.at[source], dst_ref=buffer.at[source], send_sem=send_sem.at[o],
                recv_sem=recv_sem.at[source],
                device_id=(source, part), device_id_type=MESH,
            ).wait_recv()

    def spread_parts(buffer, send_sem, recv_sem):
        copies = []
        for o in range(1, parts):
            copy = pltpu.make_async_remote_copy(
                src_ref=buffer.at[part], dst_ref=buffer.at[part], send_sem=send_sem.at[o],
                recv_sem=recv_sem.at[part],
                device_id=(own, lax.rem(part + o, parts)), device_id_type=MESH,
            )
            copy.start()
            copies.append(copy)
        return copies

    def await_parts(buffer, send_sem, recv_sem):
        for o in range(1, parts):
            source = lax.rem(part + o, parts)
            pltpu.make_async_remote_copy(
                src_ref=buffer.at[source], dst_ref=buffer.at[source], send_sem=send_sem.at[o],
                recv_sem=recv_sem.at[source],
                device_id=(own, source), device_id_type=MESH,
            ).wait_recv()

    clean = group_softmax(logits, first)
    use_all[own] = jnp.sum(clean, axis=0, keepdims=True)

    loads[5].wait()
    ctx_f = ctxt[...].astype(jnp.float32)
    ctx = ctx_f.T.astype(jnp.bfloat16)
    tgt_f = own_t[...].astype(jnp.float32)
    row_self = jnp.sum(ctx_f * tgt_f, axis=0, keepdims=True)
    row_norm = jnp.sum(tgt_f * tgt_f, axis=0, keepdims=True)
    row_ctx = jnp.sum(ctx_f * ctx_f, axis=0, keepdims=True)
    loads[6].wait()
    loads[7].wait()
    picks = jnp.concatenate(
        [jnp.zeros((1, count), jnp.int32), dist[...], jnp.zeros((LANES - neg - 1, count), jnp.int32)], axis=0
    ).astype(jnp.float32).T.astype(jnp.int32)
    owner = picks // count
    local = picks - owner * count
    distance = owner - own
    distance = jnp.where(distance < 0, distance + shards, distance)

    norms = [None] * len(offsets)
    dots = jnp.zeros((count, LANES), jnp.float32)
    last = 0
    for j in (2, 1, 5, 4, 3, last):
        arrivals[j].wait_recv()
        block = nb[j]
        block_f = block.astype(jnp.float32)
        norms[j] = jnp.sum(block_f * block_f, axis=0, keepdims=True)
        if j == last:
            rows = [row_self, row_norm, row_ctx] + norms
            rows += [jnp.zeros((1, count), jnp.float32)] * (rows_all.shape[1] - len(rows))
            rows_all[part] = jnp.concatenate(rows, axis=0)
            sends += spread_parts(rows_all, r_send, r_recv)
        sims = jnp.dot(ctx, block, preferred_element_type=jnp.float32)
        taken = jnp.take_along_axis(sims, local, axis=1)
        dots = jnp.where(distance == distances[j], taken, dots)
    dots_all[part] = dots.astype(jnp.bfloat16)
    sends += spread_parts(dots_all, d_send, d_recv)
    sends += spread_frames(use_all, u_send, u_recv)

    await_parts(rows_all, r_send, r_recv)
    rows_sum = rows_all[0]
    for p in range(1, parts):
        rows_sum = rows_sum + rows_all[p]
    inverse = lax.rsqrt(rows_sum + norm_epsilon)
    scale = jnp.zeros((count, LANES), jnp.float32)
    for j, d in enumerate(distances):
        table = jnp.broadcast_to(inverse[3 + j : 4 + j], (count, LANES))
        taken = jnp.take_along_axis(table, local, axis=1)
        scale = jnp.where(distance == d, taken, scale)

    await_parts(dots_all, d_send, d_recv)
    dots_sum = dots_all[0].astype(jnp.float32)
    for p in range(1, parts):
        dots_sum = dots_sum + dots_all[p].astype(jnp.float32)
    gain = inverse[2:3] / logit_softness
    row = lax.broadcasted_iota(jnp.int32, (LANES, count), 0)
    first_row = rows_sum[0:1] * inverse[1:2] * gain
    found = jnp.where(row == 0, first_row, (dots_sum * scale).T * gain)
    scores_o[...] = found[: neg + 1]
    total = jnp.sum(jnp.where(row <= neg, jnp.exp(found), 0.0), axis=0, keepdims=True)
    cross = jnp.log(total) - first_row
    ce_all[own] = jnp.where(mask[...] == 1, cross, 0.0)
    sends += spread_frames(ce_all, c_send, c_recv)

    await_frames(use_all, u_send, u_recv)
    frames_all = count * shards
    usage = use_all[0]
    for s in range(1, shards):
        usage = usage + use_all[s]
    usage = usage / frames_all
    entropy = usage * jnp.log(usage + 1e-07)
    in_first = lax.broadcasted_iota(jnp.int32, (1, wide), 1) < V
    ent0 = jnp.sum(jnp.where(in_first, entropy, 0.0), axis=1, keepdims=True)
    ent1 = jnp.sum(jnp.where(in_first, 0.0, entropy), axis=1, keepdims=True)
    perplex = jnp.exp(-ent0) + jnp.exp(-ent1)
    pair_o[1] = jnp.sum((wide - perplex) / wide)

    await_frames(ce_all, c_send, c_recv)
    losses = ce_all[0]
    for s in range(1, shards):
        losses = losses + ce_all[s]
    pair_o[0] = jnp.sum(losses) / frames_all
    for copy in sends:
        copy.wait_send()


def on_device(shards, parts, features, logit_weight, gumbel, codebook, project_weight, context, distractors, masked):
    count, neg = distractors.shape
    width = context.shape[1]
    wide = logit_weight.shape[1]
    bf16, f32 = jnp.bfloat16, jnp.float32
    operands = (
        features, logit_weight, gumbel, codebook, project_weight.T, context.T, distractors.T,
        masked.reshape(1, count),
    )
    dma = pltpu.SemaphoreType.DMA
    scores, both = pl.pallas_call(
        functools.partial(kernel, shards, parts),
        out_shape=(
            pltpu.VMEM((neg + 1, count), f32),
            pltpu.SMEM((2,), f32),
        ),
        in_specs=[pl.BlockSpec(memory_space=pl.ANY)] * len(operands),
        out_specs=(
            pl.BlockSpec(memory_space=pltpu.VMEM),
            pl.BlockSpec(memory_space=pltpu.SMEM),
        ),
        scratch_shapes=[pltpu.VMEM(x.shape, x.dtype) for x in operands]
        + [
            dma((len(operands),)),
            pltpu.VMEM((width, count), bf16),
            pltpu.VMEM((2 * REACH, width, count), bf16), dma((2 * REACH,)), dma((2 * REACH,)),
            pltpu.VMEM((shards, 1, wide), f32), dma((shards,)), dma((shards,)),
            pltpu.VMEM((parts, count, LANES), bf16), dma((parts,)), dma((parts,)),
            pltpu.VMEM((parts, 16, count), f32), dma((parts,)), dma((parts,)),
            pltpu.VMEM((shards, 1, count), f32), dma((shards,)), dma((shards,)),
        ],
        compiler_params=pltpu.CompilerParams(collective_id=0, has_side_effects=True),
    )(*operands)
    return scores.T, both[0], both[1]


def solution(mesh):
    return jax.shard_map(
        functools.partial(on_device, mesh.shape["frames"], mesh.shape["mp"]),
        mesh=mesh,
        in_specs=(
            P("frames", None),
            P(),
            P("frames", None),
            P(),
            P(None, "mp"),
            P("frames", "mp"),
            P("frames", None),
            P("frames"),
        ),
        out_specs=(P("frames", None), P(), P()),
        check_vma=False,
    )
```
